512 devices in a mesh: row: 16 (over y_hi, x), blk: 32 (over y_lo, z, core).
Axes of the slice: x: 4, y: 8 (y_hi: 4, y_lo: 2; y = y_hi * 2 + y_lo), z: 8, core: 2. Of those that a mesh axis runs over, the one named last changes fastest.
Arguments:
- features: bfloat16 [131072, 512], P(('row', 'blk')), may hold values from -6 to 6
- edge_tiles: bfloat16 [16, 32, 48, 128, 128], P('row', 'blk'), may hold values from 0 to 1
- tile_src: int32 [16, 32, 48], P('row', 'blk'), may hold values from 0 to 63, as said below
- tile_dst: int32 [16, 32, 48], P('row', 'blk'), may hold values from 0 to 31
- tile_count: int32 [16, 32], P('row', 'blk'), may hold values from 9 to 48, as said below
- weight: bfloat16 [1024, 512], replicated, may hold values from -0.25 to 0.25
- out_bias: float32 [512], replicated, may hold values from -3 to 3
Outputs:
- exposure: bfloat16 [131072, 512], P(('row', 'blk'))
The draws below stay inside these ranges and needn't reach their ends.
Inputs may be any that keep to these rules, and one draw needn't show every extreme that they name: `tile_count`: live slots of a device; the busiest device has all 48. `tile_src`: the live entries of each device ascend; source block s lies at loop position s // 2, which may be any position of the closed loop of 32 positions.
All inputs are finite; a program needn't handle non-finite values.
Results may differ from the reference program's by a relative error of at most 0.006.
Values may be sent and summed in bfloat16 or wider, within the bound.
No kernel may reach another device: no remote copies, remote signals or barrier semaphores. Data moves between devices by JAX's collectives and lax.ppermute only.
A program may use at most 128 MiB of HBM per device.

```python
import math
import jax
import jax.numpy as jnp
from jax import lax

F = 512
BLOCK = 128
NB = 2
TILES_DEV = 48
GROUPS = 16
LOOP = 32
REACH = 16
NODES = 131072


def count_helper(key):
    divisor = jax.random.randint(jax.random.fold_in(key, 11), (GROUPS * LOOP,), 1, 6)
    counts = jnp.maximum(TILES_DEV // divisor, 2)
    chosen = jax.random.randint(jax.random.fold_in(key, 12), (), 0, GROUPS * LOOP)
    counts = jnp.where(jnp.arange(GROUPS * LOOP) == chosen, TILES_DEV, counts)
    return counts.reshape(GROUPS, LOOP).astype(jnp.int32)


def draw_tile_count(key, part):
    return count_helper(key)


def draw_tile_src(key, part):
    shape = (GROUPS, LOOP, TILES_DEV)
    offsets = jax.random.randint(jax.random.fold_in(key, 31), shape, -REACH, REACH + 1)
    slot_ids = jnp.arange(TILES_DEV)[None, None, :]
    offsets = jnp.where(slot_ids == 0, -REACH, jnp.where(slot_ids == 1, REACH, offsets))
    inner = jax.random.randint(jax.random.fold_in(key, 32), shape, 0, NB)
    position = (jnp.arange(LOOP)[None, :, None] + offsets) % LOOP
    sources = position * NB + inner
    counts = count_helper(key)
    live_slot = slot_ids < counts[:, :, None]
    ranked = jnp.where(live_slot, 0, LOOP * NB) + sources
    ordered = jnp.sort(ranked, axis=-1) % (LOOP * NB)
    return ordered.astype(jnp.int32)


def draw_edge_tiles(key, part):
    shape = (GROUPS, LOOP, TILES_DEV, BLOCK, BLOCK)
    activity = jnp.exp(jax.random.uniform(jax.random.fold_in(key, 21), (BLOCK,), jnp.float32, math.log(0.01), 0.0))
    picker = jax.random.uniform(jax.random.fold_in(key, 22), shape, jnp.float32)
    values = jnp.exp(jax.random.uniform(jax.random.fold_in(key, 23), shape, jnp.float32, math.log(0.1), 0.0))
    present = picker < 0.03 * activity[None, None, None, :, None]
    weights = jnp.where(present, values, 0.0)
    counts = count_helper(key)
    slot_ids = jnp.arange(TILES_DEV)[None, None, :, None, None]
    filled = jnp.where(slot_ids < counts[:, :, None, None, None], weights, 1.0 - picker)
    return filled.astype(jnp.bfloat16)


def place_ends(values, own_key, least, top_value):
    longest = values.shape.index(max(values.shape))
    spots = []
    for shift in (0, 1):
        where = [jax.random.randint(jax.random.fold_in(own_key, axis), (), 0, length) for axis, length in enumerate(values.shape)]
        where[longest] = (where[longest] + shift) % values.shape[longest]
        spots.append(tuple(where))
    return values.at[spots[0]].set(least).at[spots[1]].set(top_value)


def shard_levels(stream_key, extent, shards, least, top_value):
    factor_of = 1.0
    for axis_at, shards_of in shards:
        heights = jax.random.uniform(jax.random.fold_in(jax.random.fold_in(stream_key, 6), axis_at), (shards_of,), jnp.float32, least / len(shards), top_value / len(shards))
        factor_of = factor_of * jnp.repeat(jnp.exp(heights), extent[axis_at] // shards_of).reshape((-1,) + (1,) * (len(extent) - 1 - axis_at))
    return factor_of


def bell_draw(key, extent, width, limit, cuts=(), kind=jnp.bfloat16):
    values = jax.random.normal(key, extent, jnp.float32) * width
    if len(cuts) > 0:
        values = shard_levels(key, extent, cuts, -0.22, 0.18) * values
    return jnp.clip(values, min=-limit, max=limit).astype(kind)


def setup_inputs(seed: int = 0) -> dict:
    arg_keys = jax.random.split(jax.random.key(seed), 8)
    return {
        "features": bell_draw(arg_keys[0], (NODES, F), 1.0, 6.0, ((0, 512),)),
        "edge_tiles": draw_edge_tiles(jax.random.fold_in(arg_keys[7], 71), 0),
        "tile_src": draw_tile_src(jax.random.fold_in(arg_keys[7], 71), 0),
        "tile_dst": place_ends(jax.random.randint(arg_keys[3], (GROUPS, LOOP, TILES_DEV), 0, GROUPS * NB), jax.random.fold_in(arg_keys[3], 1), 0, (GROUPS * NB) - 1).astype(jnp.int32),
        "tile_count": draw_tile_count(jax.random.fold_in(arg_keys[7], 71), 0),
        "weight": bell_draw(arg_keys[5], (2 * F, F), F ** -0.5, 0.25),
        "out_bias": bell_draw(arg_keys[6], (F,), 0.5, 3.0, (), jnp.float32),
    }


def reference(features, edge_tiles, tile_src, tile_dst, tile_count, weight, out_bias):
    tile_width = edge_tiles.shape[-1]
    feat_width = features.shape[1]
    dest_blocks = GROUPS * NB
    feat_blocks = features.reshape(GROUPS, LOOP * NB, tile_width, feat_width)
    block_ids = jnp.arange(dest_blocks, dtype=jnp.int32)
    slot_ids = jnp.arange(TILES_DEV, dtype=jnp.int32)

    def device_step(carry, index):
        totals, degrees = carry
        group = index // LOOP
        column = index % LOOP
        tiles_here = edge_tiles[group, column]
        sources = tile_src[group, column]
        targets = tile_dst[group, column]
        live_slot = slot_ids < tile_count[group, column]
        gathered = feat_blocks[group][sources]
        products = jnp.einsum("tij,tjf->tif", tiles_here.astype(jnp.float32), gathered.astype(jnp.float32), precision=lax.Precision.HIGHEST)
        selector = ((targets[None, :] == block_ids[:, None]) & live_slot[None, :]).astype(jnp.float32)
        partial_value = jnp.einsum("qt,tif->qif", selector, products, precision=lax.Precision.HIGHEST).astype(jnp.bfloat16)
        row_sums = jnp.sum(tiles_here, axis=2, dtype=jnp.float32)
        partial_degree = jnp.dot(selector, row_sums, precision=lax.Precision.HIGHEST).astype(jnp.bfloat16)
        totals = totals.at[column].add(partial_value.astype(jnp.float32))
        degrees = degrees.at[column].add(partial_degree.astype(jnp.float32))
        return (totals, degrees), None

    start_totals = jnp.zeros((LOOP, dest_blocks, tile_width, feat_width), jnp.float32)
    start_degrees = jnp.zeros((LOOP, dest_blocks, tile_width), jnp.float32)
    (totals, degrees), unused = lax.scan(device_step, (start_totals, start_degrees), jnp.arange(GROUPS * LOOP, dtype=jnp.int32))
    aggregate = totals.reshape(LOOP, GROUPS, NB, tile_width, feat_width).transpose(1, 0, 2, 3, 4).reshape(-1, feat_width)
    degree = degrees.reshape(LOOP, GROUPS, NB, tile_width).transpose(1, 0, 2, 3).reshape(-1)
    neighbor_mean = (aggregate / jnp.maximum(degree, 1.0)[:, None]).astype(jnp.bfloat16)
    joined = jnp.concatenate([features, neighbor_mean], axis=1)
    mixed = jnp.dot(joined, weight, preferred_element_type=jnp.float32) + out_bias
    return jax.nn.relu(mixed).astype(jnp.bfloat16)
```

```python
import jax
import jax.numpy as jnp
from jax import lax
from jax.experimental import pallas as pl
from jax.experimental.pallas import tpu as pltpu
from jax.sharding import PartitionSpec as P

UNROLL = 4


def scatter_matmul(table, tiles, source_ids, target_ids, live_count, dest_blocks):
    slot_total, tile_width, unused = tiles.shape
    feat_width = table.shape[-1]

    def kernel(src_ref, dst_ref, count_ref, table_ref, tiles_ref, out_ref, total_ref):
        count = count_ref[0]

        def clear(block, carry):
            total_ref[block] = jnp.zeros((tile_width, feat_width), jnp.float32)
            return carry

        lax.fori_loop(0, dest_blocks, clear, 0)

        def some_slots(index, carry):
            products = []
            for step in range(UNROLL):
                slot = index * UNROLL + step
                products.append(
                    jnp.dot(
                        tiles_ref[slot],
                        table_ref[src_ref[slot]],
                        preferred_element_type=jnp.float32,
                    )
                )
            for step in range(UNROLL):
                slot = index * UNROLL + step
                target = jnp.where(slot < count, dst_ref[slot], dest_blocks)
                total_ref[target] += products[step]
            return carry

        lax.fori_loop(0, pl.cdiv(count, UNROLL), some_slots, 0)

        def round_once(block, carry):
            out_ref[block] = total_ref[block].astype(jnp.bfloat16)
            return carry

        lax.fori_loop(0, dest_blocks, round_once, 0)

    smem = pl.BlockSpec(memory_space=pltpu.SMEM)
    vmem = pl.BlockSpec(memory_space=pltpu.VMEM)
    return pl.pallas_call(
        kernel,
        name="scatter_matmul",
        out_shape=jax.ShapeDtypeStruct((dest_blocks, tile_width, feat_width), jnp.bfloat16),
        in_specs=[smem, smem, smem, vmem, vmem],
        out_specs=vmem,
        scratch_shapes=[pltpu.VMEM((dest_blocks + 1, tile_width, feat_width), jnp.float32)],
        cost_estimate=pl.CostEstimate(
            flops=2 * slot_total * tile_width * tile_width * feat_width,
            bytes_accessed=table.size * 2 + tiles.size * 2 + dest_blocks * tile_width * feat_width * 2,
            transcendentals=0,
        ),
        compiler_params=pltpu.CompilerParams(vmem_limit_bytes=40 * 1024 * 1024),
    )(source_ids, target_ids, live_count, table, tiles)


def per_device(features, edge_tiles, tile_src, tile_dst, tile_count, weight, out_bias):
    tiles_here = edge_tiles[0, 0]
    source_ids = tile_src[0, 0]
    target_ids = tile_dst[0, 0]
    live_count = tile_count[0]
    slot_total = tiles_here.shape[0]
    tile_width = tiles_here.shape[-1]
    node_rows, feat_width = features.shape
    group_count = lax.axis_size("row")
    dest_blocks = group_count * node_rows // tile_width
    live_slot = jnp.arange(slot_total, dtype=jnp.int32) < live_count[0]

    table = lax.all_gather(features, "blk", axis=0, tiled=True)

    row_sums = jnp.sum(tiles_here, axis=2, dtype=jnp.float32)
    block_ids = jnp.arange(dest_blocks, dtype=jnp.int32)
    selector = ((target_ids[None, :] == block_ids[:, None]) & live_slot[None, :]).astype(jnp.float32)
    degree_part = jnp.dot(selector, row_sums, precision=lax.Precision.HIGHEST)
    degree_parts = lax.all_to_all(
        degree_part.astype(jnp.bfloat16).reshape(group_count, node_rows), "row", 0, 0
    )
    degree = jnp.sum(degree_parts.astype(jnp.float32), axis=0)
    own_part = jnp.dot(features, weight[:feat_width], preferred_element_type=jnp.float32) + out_bias

    partial = scatter_matmul(
        table.reshape(-1, tile_width, feat_width), tiles_here, source_ids, target_ids, live_count, dest_blocks
    )
    aggregate = lax.psum_scatter(
        partial.reshape(-1, feat_width), "row", scatter_dimension=0, tiled=True
    ).astype(jnp.float32)
    neighbor_mean = (aggregate / jnp.maximum(degree, 1.0)[:, None]).astype(jnp.bfloat16)
    mixed = jnp.dot(neighbor_mean, weight[feat_width:], preferred_element_type=jnp.float32) + own_part
    return jax.nn.relu(mixed).astype(jnp.bfloat16)


def solution(mesh):
    in_specs = (
        P(("row", "blk"), None),
        P("row", "blk", None, None, None),
        P("row", "blk", None),
        P("row", "blk", None),
        P("row", "blk"),
        P(),
        P(),
    )
    return jax.shard_map(
        per_device, mesh=mesh, in_specs=in_specs, out_specs=P(("row", "blk"), None), check_vma=False
    )
```

```python
import jax
import jax.numpy as jnp
from jax import lax
from jax.experimental import pallas as pl
from jax.experimental.pallas import tpu as pltpu
from jax.sharding import PartitionSpec as P


UNROLL = 4
SIDE = 4
FIRST = 176


def partial_sums(table, tiles, source_ids, target_ids, live_count, place, owner_rows):
    slot_total, tile_width, unused = tiles.shape
    feat_width = table.shape[-1]
    owner_blocks = owner_rows // tile_width
    dest_blocks = SIDE * SIDE * owner_blocks
    parts = (("x", 0, FIRST), ("y", FIRST, owner_rows))

    def kernel(src_ref, dst_ref, count_ref, place_ref, table_ref, tiles_ref, *refs):
        outs, total_ref = refs[:-1], refs[-1]
        count = count_ref[0]

        def clear(block, carry):
            total_ref[block] = jnp.zeros((tile_width, feat_width), jnp.float32)
            return carry

        lax.fori_loop(0, dest_blocks, clear, 0)

        def some_slots(index, carry):
            products = []
            for step in range(UNROLL):
                slot = index * UNROLL + step
                products.append(
                    jnp.dot(tiles_ref[slot], table_ref[src_ref[slot]], preferred_element_type=jnp.float32)
                )
            for step in range(UNROLL):
                slot = index * UNROLL + step
                target = jnp.where(slot < count, dst_ref[slot], dest_blocks)
                total_ref[target] += products[step]
            return carry

        lax.fori_loop(0, pl.cdiv(count, UNROLL), some_slots, 0)

        x, y = place_ref[0], place_ref[1]
        for shift in range(SIDE):

            def round_once(other, carry):
                for at, (axis, first, last) in enumerate(parts):
                    owner_x = lax.rem(x + (shift if axis == "x" else other), SIDE)
                    owner_y = lax.rem(y + (other if axis == "x" else shift), SIDE)
                    block = (owner_y * SIDE + owner_x) * owner_blocks
                    out_ref = outs[at * SIDE + shift]
                    for inner in range(owner_blocks):
                        low, high = max(first, inner * tile_width), min(last, (inner + 1) * tile_width)
                        if low < high:
                            out_ref[other, low - first : high - first] = total_ref[
                                block + inner, low - inner * tile_width : high - inner * tile_width
                            ].astype(jnp.bfloat16)
                return carry

            lax.fori_loop(0, SIDE, round_once, 0)

    smem = pl.BlockSpec(memory_space=pltpu.SMEM)
    vmem = pl.BlockSpec(memory_space=pltpu.VMEM)
    out_shape = [
        jax.ShapeDtypeStruct((SIDE, last - first, feat_width), jnp.bfloat16)
        for unused, first, last in parts
        for shift in range(SIDE)
    ]
    outs = pl.pallas_call(
        kernel,
        name="partial_sums",
        out_shape=out_shape,
        in_specs=[smem, smem, smem, smem, vmem, vmem],
        out_specs=[vmem] * len(out_shape),
        scratch_shapes=[pltpu.VMEM((dest_blocks + 1, tile_width, feat_width), jnp.float32)],
        cost_estimate=pl.CostEstimate(
            flops=2 * slot_total * tile_width * tile_width * feat_width,
            bytes_accessed=table.size * 2 + tiles.size * 2 + dest_blocks * tile_width * feat_width * 2,
            transcendentals=0,
        ),
        compiler_params=pltpu.CompilerParams(vmem_limit_bytes=40 * 1024 * 1024),
    )(source_ids, target_ids, live_count, place, table, tiles)
    return outs[:SIDE], outs[SIDE:]


def along_x(value, shift):
    pairs = [(i, i // SIDE * SIDE + (i % SIDE + shift) % SIDE) for i in range(SIDE * SIDE)]
    return lax.ppermute(value, "row", pairs)


def along_y(value, shift):
    pairs = [(i, (i // SIDE + shift) % SIDE * SIDE + i % SIDE) for i in range(SIDE * SIDE)]
    return lax.ppermute(value, "row", pairs)


def reduce_scatter(first_parts, second_parts):
    order = (2, 1, 3)
    wide = jnp.float32
    got_x = {shift: along_x(first_parts[shift], shift) for shift in order}
    got_y = {shift: along_y(second_parts[shift], shift) for shift in order}

    def total(own, got, at):
        return own[at].astype(wide) + (
            (got[1][at].astype(wide) + got[3][at].astype(wide)) + got[2][at].astype(wide)
        )

    sums_x = [total(first_parts[0], got_x, at) for at in range(SIDE)]
    sums_y = [total(second_parts[0], got_y, at) for at in range(SIDE)]
    narrow = jnp.bfloat16
    then_y = [along_y(sums_x[shift].astype(narrow), shift).astype(wide) for shift in order]
    then_x = [along_x(sums_y[shift].astype(narrow), shift).astype(wide) for shift in order]
    return jnp.concatenate([sum(then_y, sums_x[0]), sum(then_x, sums_y[0])], axis=0)


def per_device(features, edge_tiles, tile_src, tile_dst, tile_count, weight, out_bias):
    tiles_here = edge_tiles[0, 0]
    source_ids = tile_src[0, 0]
    target_ids = tile_dst[0, 0]
    live_count = tile_count[0]
    slot_total = tiles_here.shape[0]
    tile_width = tiles_here.shape[-1]
    node_rows, feat_width = features.shape
    group_count = lax.axis_size("row")
    dest_blocks = group_count * node_rows // tile_width
    live_slot = jnp.arange(slot_total, dtype=jnp.int32) < live_count[0]

    table = lax.all_gather(features, "blk", axis=0, tiled=True)

    row_sums = jnp.sum(tiles_here, axis=2, dtype=jnp.float32)
    block_ids = jnp.arange(dest_blocks, dtype=jnp.int32)
    selector = ((target_ids[None, :] == block_ids[:, None]) & live_slot[None, :]).astype(jnp.float32)
    degree_part = jnp.dot(selector, row_sums, precision=lax.Precision.HIGHEST)
    degree_parts = lax.all_to_all(
        degree_part.astype(jnp.bfloat16).reshape(group_count, node_rows), "row", 0, 0
    )
    degree = jnp.sum(degree_parts.astype(jnp.float32), axis=0)
    own_part = jnp.dot(features, weight[:feat_width], preferred_element_type=jnp.float32) + out_bias
    me = lax.axis_index("row")
    place = jnp.stack([me % SIDE, me // SIDE]).astype(jnp.int32)
    place, degree, own_part = lax.optimization_barrier((place, degree, own_part))

    first_parts, second_parts = partial_sums(
        table.reshape(-1, tile_width, feat_width),
        tiles_here,
        source_ids,
        target_ids,
        live_count,
        place,
        node_rows,
    )
    aggregate = reduce_scatter(first_parts, second_parts)
    neighbor_mean = (aggregate / jnp.maximum(degree, 1.0)[:, None]).astype(jnp.bfloat16)
    mixed = jnp.dot(neighbor_mean, weight[feat_width:], preferred_element_type=jnp.float32) + own_part
    return jax.nn.relu(mixed).astype(jnp.bfloat16)


def solution(mesh):
    in_specs = (
        P(("row", "blk"), None),
        P("row", "blk", None, None, None),
        P("row", "blk", None),
        P("row", "blk", None),
        P("row", "blk"),
        P(),
        P(),
    )
    return jax.shard_map(
        per_device, mesh=mesh, in_specs=in_specs, out_specs=P(("row", "blk"), None), check_vma=False
    )
```

```python
import jax
import jax.numpy as jnp
from jax import lax
from jax.experimental import pallas as pl
from jax.experimental.pallas import tpu as pltpu
from jax.sharding import PartitionSpec as P


UNROLL = 4
SIDE = 4
FIRST = 176


def partial_sums(table, tiles, source_ids, target_ids, live_count, owner_rows):
    slot_total, tile_width, unused = tiles.shape
    feat_width = table.shape[-1]
    owner_blocks = owner_rows // tile_width
    dest_blocks = SIDE * SIDE * owner_blocks

    def kernel(src_ref, dst_ref, count_ref, table_ref, tiles_ref, *refs):
        outs, total_ref = refs[:-1], refs[-1]
        count = count_ref[0]

        def clear(block, carry):
            total_ref[block] = jnp.zeros((tile_width, feat_width), jnp.float32)
            return carry

        lax.fori_loop(0, dest_blocks, clear, 0)

        def some_slots(index, carry):
            products = []
            for step in range(UNROLL):
                slot = index * UNROLL + step
                products.append(
                    jnp.dot(tiles_ref[slot], table_ref[src_ref[slot]], preferred_element_type=jnp.float32)
                )
            for step in range(UNROLL):
                slot = index * UNROLL + step
                target = jnp.where(slot < count, dst_ref[slot], dest_blocks)
                total_ref[target] += products[step]
            return carry

        lax.fori_loop(0, pl.cdiv(count, UNROLL), some_slots, 0)

        def round_once(owner, carry):
            x, y = lax.rem(owner, SIDE), lax.div(owner, SIDE)
            for out_ref, at, (low, high) in ((outs[0], (x, y), (0, FIRST)), (outs[1], (y, x), (FIRST, owner_rows))):
                for inner in range(owner_blocks):
                    first, last = max(low, inner * tile_width), min(high, (inner + 1) * tile_width)
                    if first < last:
                        out_ref[at + (slice(first - low, last - low),)] = total_ref[
                            owner * owner_blocks + inner, first - inner * tile_width : last - inner * tile_width
                        ].astype(jnp.bfloat16)
            return carry

        lax.fori_loop(0, SIDE * SIDE, round_once, 0)

    smem = pl.BlockSpec(memory_space=pltpu.SMEM)
    vmem = pl.BlockSpec(memory_space=pltpu.VMEM)
    out_shape = [
        jax.ShapeDtypeStruct((SIDE, SIDE, rows, feat_width), jnp.bfloat16) for rows in (FIRST, owner_rows - FIRST)
    ]
    return pl.pallas_call(
        kernel,
        name="partial_sums",
        out_shape=out_shape,
        in_specs=[smem, smem, smem, vmem, vmem],
        out_specs=[vmem] * len(out_shape),
        scratch_shapes=[pltpu.VMEM((dest_blocks + 1, tile_width, feat_width), jnp.float32)],
        cost_estimate=pl.CostEstimate(
            flops=2 * slot_total * tile_width * tile_width * feat_width,
            bytes_accessed=table.size * 2 + tiles.size * 2 + dest_blocks * tile_width * feat_width * 2,
            transcendentals=0,
        ),
        compiler_params=pltpu.CompilerParams(vmem_limit_bytes=40 * 1024 * 1024),
    )(source_ids, target_ids, live_count, table, tiles)


def exchange(value, axis):
    if axis == "x":
        groups = [[y * SIDE + x for x in range(SIDE)] for y in range(SIDE)]
    else:
        groups = [[y * SIDE + x for y in range(SIDE)] for x in range(SIDE)]
    return lax.all_to_all(value, "row", 0, 0, axis_index_groups=groups)


def total(parts):
    return jnp.sum(parts.astype(jnp.float32), axis=0)


def reduce_scatter(first_part, second_part):
    first = total(exchange(first_part, "x")).astype(jnp.bfloat16)
    second = total(exchange(second_part, "y")).astype(jnp.bfloat16)
    first = total(exchange(first, "y"))
    second = total(exchange(second, "x"))
    return jnp.concatenate([first, second], axis=0)


def per_device(features, edge_tiles, tile_src, tile_dst, tile_count, weight, out_bias):
    tiles_here = edge_tiles[0, 0]
    source_ids = tile_src[0, 0]
    target_ids = tile_dst[0, 0]
    live_count = tile_count[0]
    slot_total = tiles_here.shape[0]
    tile_width = tiles_here.shape[-1]
    node_rows, feat_width = features.shape
    group_count = lax.axis_size("row")
    dest_blocks = group_count * node_rows // tile_width
    live_slot = jnp.arange(slot_total, dtype=jnp.int32) < live_count[0]

    table = lax.all_gather(features, "blk", axis=0, tiled=True)

    row_sums = jnp.sum(tiles_here, axis=2, dtype=jnp.float32)
    block_ids = jnp.arange(dest_blocks, dtype=jnp.int32)
    selector = ((target_ids[None, :] == block_ids[:, None]) & live_slot[None, :]).astype(jnp.float32)
    degree_part = jnp.dot(selector, row_sums, precision=lax.Precision.HIGHEST)
    degree_parts = lax.all_to_all(
        degree_part.astype(jnp.bfloat16).reshape(group_count, node_rows), "row", 0, 0
    )
    degree = jnp.sum(degree_parts.astype(jnp.float32), axis=0)
    own_part = jnp.dot(features, weight[:feat_width], preferred_element_type=jnp.float32) + out_bias
    source_ids, degree, own_part = lax.optimization_barrier((source_ids, degree, own_part))

    first_part, second_part = partial_sums(
        table.reshape(-1, tile_width, feat_width),
        tiles_here,
        source_ids,
        target_ids,
        live_count,
        node_rows,
    )
    aggregate = reduce_scatter(first_part, second_part)
    neighbor_mean = (aggregate / jnp.maximum(degree, 1.0)[:, None]).astype(jnp.bfloat16)
    mixed = jnp.dot(neighbor_mean, weight[feat_width:], preferred_element_type=jnp.float32) + own_part
    return jax.nn.relu(mixed).astype(jnp.bfloat16)


def solution(mesh):
    in_specs = (
        P(("row", "blk"), None),
        P("row", "blk", None, None, None),
        P("row", "blk", None),
        P("row", "blk", None),
        P("row", "blk"),
        P(),
        P(),
    )
    return jax.shard_map(
        per_device, mesh=mesh, in_specs=in_specs, out_specs=P(("row", "blk"), None), check_vma=False
    )
```

```python
import jax
import jax.numpy as jnp
from jax import lax
from jax.experimental import pallas as pl
from jax.experimental.pallas import tpu as pltpu
from jax.sharding import PartitionSpec as P


UNROLL = 4
SIDE, PAIR, RING = 4, 2, 8
FIRST = 192


def partial_sums(table, tile_sets, sources, targets, counts, x, owner_rows):
    slot_total, tile_width, unused = tile_sets[0].shape
    feat_width = table.shape[-1]
    owner_blocks = owner_rows // tile_width
    dest_blocks = SIDE * SIDE * PAIR * owner_blocks

    def kernel(src_ref, dst_ref, count_ref, x_ref, table_ref, own_ref, other_ref, *refs):
        outs, total_ref = refs[:-1], refs[-1]

        def clear(block, carry):
            total_ref[block] = jnp.zeros((tile_width, feat_width), jnp.float32)
            return carry

        lax.fori_loop(0, dest_blocks, clear, 0)

        for at, tiles_ref in enumerate((own_ref, other_ref)):

            def some_slots(index, carry):
                slots = [index * UNROLL + step for step in range(UNROLL)]
                products = [
                    jnp.dot(tiles_ref[slot], table_ref[src_ref[at, slot]], preferred_element_type=jnp.float32)
                    for slot in slots
                ]
                for slot, product in zip(slots, products):
                    total_ref[dst_ref[at, slot]] += product
                return carry

            lax.fori_loop(0, pl.cdiv(count_ref[at], UNROLL), some_slots, 0)

        def round_once(step, carry):
            owner_y, shift = lax.div(step, SIDE), lax.rem(step, SIDE)
            owner_x = lax.rem(x_ref[0] + shift, SIDE)
            y_hi, y_lo = lax.div(owner_y, PAIR), lax.rem(owner_y, PAIR)
            block = (y_lo * SIDE * SIDE + y_hi * SIDE + owner_x) * owner_blocks
            rows = jnp.concatenate(
                [total_ref[block + inner].astype(jnp.bfloat16) for inner in range(owner_blocks)], axis=0
            )
            for static in range(SIDE):

                @pl.when(shift == static)
                def _():
                    outs[static][owner_y] = rows[:FIRST]

            outs[SIDE][owner_y, shift] = rows[FIRST:]
            return carry

        lax.fori_loop(0, SIDE * SIDE * PAIR, round_once, 0)

    smem = pl.BlockSpec(memory_space=pltpu.SMEM)
    vmem = pl.BlockSpec(memory_space=pltpu.VMEM)
    out_shape = [jax.ShapeDtypeStruct((SIDE * PAIR, FIRST, feat_width), jnp.bfloat16)] * SIDE
    out_shape.append(jax.ShapeDtypeStruct((SIDE * PAIR, SIDE, owner_rows - FIRST, feat_width), jnp.bfloat16))
    outs = pl.pallas_call(
        kernel,
        name="partial_sums",
        out_shape=out_shape,
        in_specs=[smem] * 4 + [vmem] * 3,
        out_specs=[vmem] * len(out_shape),
        scratch_shapes=[pltpu.VMEM((dest_blocks + 1, tile_width, feat_width), jnp.float32)],
        cost_estimate=pl.CostEstimate(
            flops=4 * slot_total * tile_width * tile_width * feat_width,
            bytes_accessed=table.size * 2 + tile_sets[0].size * 4 + dest_blocks * tile_width * feat_width * 2,
            transcendentals=0,
        ),
        compiler_params=pltpu.CompilerParams(vmem_limit_bytes=40 * 1024 * 1024),
    )(sources, targets, counts, x, table, *tile_sets)
    return outs[:SIDE], outs[SIDE]


def along_x(value, shift):
    pairs = [(i, i // SIDE * SIDE + (i % SIDE + shift) % SIDE) for i in range(SIDE * SIDE)]
    return lax.ppermute(value, "row", pairs)


def along_blk(value, moved):
    def index(y_lo, z, core):
        return (y_lo * RING + z % RING) * PAIR + core

    pairs = [
        (index(y_lo, z, core), index(*moved(y_lo, z, core)))
        for y_lo in range(PAIR)
        for z in range(RING)
        for core in range(PAIR)
    ]
    return lax.ppermute(value, "blk", pairs)


def to_other_y_lo(value):
    return along_blk(value, lambda y_lo, z, core: (1 - y_lo, z, core))


def to_other_core(value):
    return along_blk(value, lambda y_lo, z, core: (y_lo, z, 1 - core))


def along_z(value, shift):
    return along_blk(value, lambda y_lo, z, core: (y_lo, z + shift, core))


def exchange_y(value):
    blk_total = PAIR * RING * PAIR
    groups = [
        [(y_hi * SIDE + x) * blk_total + y_lo * RING * PAIR + rest for y_hi in range(SIDE) for y_lo in range(PAIR)]
        for x in range(SIDE)
        for rest in range(RING * PAIR)
    ]
    return lax.all_to_all(value, ("row", "blk"), 0, 0, axis_index_groups=groups)


def wide(value):
    return value.astype(jnp.float32)


def over_y_hi(parts):
    return jnp.sum(wide(parts).reshape((SIDE, PAIR) + parts.shape[1:]), axis=0)


def side_by_side(halves):
    return jnp.concatenate([halves[at] for at in range(PAIR)], axis=-1)


def reduce_scatter(first_parts, second_part):
    narrow = jnp.bfloat16
    order = (2, 1, 3)
    got_y = exchange_y(second_part)
    got_x = [along_x(first_parts[shift], shift) for shift in order]
    first = sum((wide(got) for got in got_x), wide(first_parts[0])).astype(narrow)
    first = exchange_y(first)
    second = over_y_hi(got_y)
    got_x = [along_x(second[:, shift].astype(narrow), shift) for shift in order]
    second = sum((wide(got) for got in got_x), second[:, 0])
    return jnp.concatenate([side_by_side(over_y_hi(first)), side_by_side(second)], axis=0)


def gather(features, meta, y_lo):
    node_rows, feat_width = features.shape
    half = feat_width // PAIR
    mine = lax.dynamic_slice_in_dim(features, y_lo * half, half, 1)
    theirs = lax.dynamic_slice_in_dim(features, (1 - y_lo) * half, half, 1)
    got = to_other_y_lo(jnp.concatenate([theirs, meta], axis=0))
    own = jnp.concatenate([mine, got[:node_rows]], axis=0)
    m2, p2 = along_z(own, 2), along_z(own, -2)
    m1, p1 = along_z(own, 1), along_z(own, -1)
    near = jnp.concatenate([own, p1, m1, p2, m2], axis=0)
    near_other = to_other_core(near)
    m3, p3 = along_z(m2, 1), along_z(p2, -1)
    opposite = [along_z(m2[:node_rows], 2), along_z(p2[node_rows:], -2)]
    far = jnp.concatenate([p3, m3] + opposite, axis=0)
    far_other = to_other_core(far)
    return jnp.concatenate([near, far, near_other, far_other], axis=0), got[node_rows:]


Z_ORDER = (0, 1, RING - 1, 2, RING - 2, 3, RING - 3, RING // 2)


def table_block(sources, y_lo, z, core, inner_total):
    inner, position = sources % inner_total, sources // inner_total
    place = [Z_ORDER.index(distance) for distance in range(RING)]
    away = (position // PAIR - z) % RING
    along = sum(jnp.where(away == distance, place[distance], 0) for distance in range(RING))
    other_core = position % PAIR != core
    other_y_lo = position // (PAIR * RING) != y_lo
    return ((other_core * RING + along) * PAIR + other_y_lo) * inner_total + inner


def per_device(features, edge_tiles, tile_src, tile_dst, tile_count, weight, out_bias):
    tiles_here = edge_tiles[0, 0]
    source_ids = tile_src[0, 0]
    target_ids = tile_dst[0, 0]
    live_count = tile_count[0, 0]
    slot_total = tiles_here.shape[0]
    tile_width = tiles_here.shape[-1]
    node_rows, feat_width = features.shape
    group_count = lax.axis_size("row")
    dest_blocks = group_count * node_rows // tile_width
    slot_ids = jnp.arange(slot_total, dtype=jnp.int32)
    me = lax.axis_index("blk")
    y_lo, z, core = me // (RING * PAIR), me // PAIR % RING, me % PAIR
    x = lax.axis_index("row") % SIDE

    meta = jnp.stack([source_ids, target_ids, jnp.full_like(source_ids, live_count)])
    half = feat_width // PAIR
    meta = jnp.pad(meta.astype(jnp.bfloat16), ((0, 13), (0, half - slot_total)))
    table, other_meta = gather(features, meta, y_lo)
    other_tiles = to_other_y_lo(tiles_here)
    other_meta = other_meta[:3, :slot_total].astype(jnp.int32)
    sources = jnp.stack([source_ids, other_meta[0]])
    counts = jnp.stack([live_count, other_meta[2, 0]])
    blocks_of = jnp.stack([y_lo, 1 - y_lo]) * dest_blocks
    live = slot_ids[None, :] < counts[:, None]
    targets = jnp.where(
        live, jnp.stack([target_ids, other_meta[1]]) + blocks_of[:, None], PAIR * dest_blocks
    )
    blocks = table_block(sources, y_lo, z, core, node_rows // tile_width)

    row_sums = jnp.sum(tiles_here, axis=2, dtype=jnp.float32)
    block_ids = jnp.arange(dest_blocks, dtype=jnp.int32)
    selector = (target_ids[None, :] == block_ids[:, None]) & (slot_ids < live_count)[None, :]
    degree_part = jnp.dot(selector.astype(jnp.float32), row_sums, precision=lax.Precision.HIGHEST)
    degree_parts = lax.all_to_all(
        degree_part.astype(jnp.bfloat16).reshape(group_count, node_rows), "row", 0, 0
    )
    degree = jnp.sum(degree_parts.astype(jnp.float32), axis=0)
    own_part = jnp.dot(features, weight[:feat_width], preferred_element_type=jnp.float32) + out_bias
    blocks, degree, own_part = lax.optimization_barrier((blocks, degree, own_part))

    first_parts, second_part = partial_sums(
        table.reshape(-1, tile_width, half),
        (tiles_here, other_tiles),
        blocks.astype(jnp.int32),
        targets.astype(jnp.int32),
        counts.astype(jnp.int32),
        x.astype(jnp.int32)[None],
        node_rows,
    )
    aggregate = reduce_scatter(first_parts, second_part)
    neighbor_mean = (aggregate / jnp.maximum(degree, 1.0)[:, None]).astype(jnp.bfloat16)
    mixed = jnp.dot(neighbor_mean, weight[feat_width:], preferred_element_type=jnp.float32) + own_part
    return jax.nn.relu(mixed).astype(jnp.bfloat16)


def solution(mesh):
    in_specs = (
        P(("row", "blk"), None),
        P("row", "blk", None, None, None),
        P("row", "blk", None),
        P("row", "blk", None),
        P("row", "blk"),
        P(),
        P(),
    )
    return jax.shard_map(
        per_device, mesh=mesh, in_specs=in_specs, out_specs=P(("row", "blk"), None), check_vma=False
    )
```

```python
import jax
import jax.numpy as jnp
from jax import lax
from jax.experimental import pallas as pl
from jax.experimental.pallas import tpu as pltpu
from jax.sharding import PartitionSpec as P


UNROLL = 4
SIDE, PAIR, RING = 4, 2, 8
FIRST = 192
EXTRA = 16


def partial_sums(pieces, tile_sets, sources, targets, counts, place, degrees, owner_rows):
    slot_total, tile_width, _ = tile_sets[0].shape
    feat_width = pieces[0].shape[-1]
    owner_blocks = owner_rows // tile_width
    dest_blocks = SIDE * SIDE * PAIR * owner_blocks
    pieces = [piece.reshape(-1, tile_width, feat_width) for piece in pieces]
    source_total = sum(piece.shape[0] for piece in pieces)

    def kernel(src_ref, dst_ref, count_ref, place_ref, degree_ref, *refs):
        sets, refs = refs[: len(tile_sets)], refs[len(tile_sets) :]
        piece_refs, refs = refs[: len(pieces)], refs[len(pieces) :]
        outs, (tiles_ref, table_ref, *staged, total_ref, in_sems, out_sems) = refs[: 2 * SIDE], refs[2 * SIDE :]
        loads, base = [], 0
        for piece_ref in piece_refs:
            loads.append((piece_ref, table_ref.at[pl.ds(base, piece_ref.shape[0])]))
            base += piece_ref.shape[0]
        loads += [(set_ref, tiles_ref.at[at]) for at, set_ref in enumerate(sets)]
        loads = [pltpu.make_async_copy(*pair, in_sems.at[at]) for at, pair in enumerate(loads)]
        for load in loads:
            load.start()

        def clear(block, carry):
            total_ref[block] = jnp.zeros((tile_width, feat_width), jnp.float32)
            return carry

        lax.fori_loop(0, dest_blocks, clear, 0)
        for load in loads:
            load.wait()

        for at in range(len(sets)):

            def some_slots(index, carry):
                slots = [index * UNROLL + step for step in range(UNROLL)]
                products = [
                    jnp.dot(tiles_ref[at, slot], table_ref[src_ref[at, slot]], preferred_element_type=jnp.float32)
                    for slot in slots
                ]
                for slot, product in zip(slots, products):
                    total_ref[dst_ref[at, slot]] += product
                return carry

            lax.fori_loop(0, pl.cdiv(count_ref[at], UNROLL), some_slots, 0)

        def stores(y_shift):
            pairs = [(from_ref.at[y_shift], out_ref.at[y_shift]) for from_ref, out_ref in zip(staged, outs[:SIDE])]
            pairs.append((staged[SIDE + y_shift], outs[SIDE + y_shift]))
            return [pltpu.make_async_copy(*pair, out_sems.at[y_shift, at]) for at, pair in enumerate(pairs)]

        for y_shift in range(SIDE):
            owner_y = lax.rem(place_ref[1] + y_shift, SIDE)
            for x_shift in range(SIDE):
                owner = owner_y * SIDE + lax.rem(place_ref[0] + x_shift, SIDE)
                degree_row = jnp.broadcast_to(degree_ref[owner], (EXTRA, owner_rows)).astype(jnp.bfloat16)

                def round_once(y_lo, carry, x_shift=x_shift, y_shift=y_shift, owner=owner, degree_row=degree_row):
                    block = (y_lo * SIDE * SIDE + owner) * owner_blocks
                    rows = jnp.concatenate(
                        [total_ref[block + inner].astype(jnp.bfloat16) for inner in range(owner_blocks)], axis=0
                    )
                    staged[x_shift][y_shift, y_lo] = rows[:FIRST]
                    staged[SIDE + y_shift][y_lo, x_shift, : owner_rows - FIRST] = rows[FIRST:]
                    staged[SIDE + y_shift][y_lo, x_shift, owner_rows - FIRST :] = degree_row
                    return carry

                lax.fori_loop(0, PAIR, round_once, 0)
            if y_shift > 0:
                for store in stores(y_shift - 1):
                    store.start()
        for y_shift in range(SIDE - 1):
            for store in stores(y_shift):
                store.wait()
        last = stores(SIDE - 1)
        for store in last:
            store.start()
        for store in last:
            store.wait()

    smem = pl.BlockSpec(memory_space=pltpu.SMEM)
    anywhere = pl.BlockSpec(memory_space=pl.ANY)
    hbm = pl.BlockSpec(memory_space=pltpu.HBM)
    out_shape = [jax.ShapeDtypeStruct((SIDE, PAIR, FIRST, feat_width), jnp.bfloat16)] * SIDE
    out_shape += [jax.ShapeDtypeStruct((PAIR, SIDE, owner_rows - FIRST + EXTRA, feat_width), jnp.bfloat16)] * SIDE
    outs = pl.pallas_call(
        kernel,
        name="partial_sums",
        out_shape=out_shape,
        in_specs=[smem] * 4 + [pl.BlockSpec(memory_space=pltpu.VMEM)] + [anywhere] * (len(tile_sets) + len(pieces)),
        out_specs=[hbm] * len(out_shape),
        scratch_shapes=[
            pltpu.VMEM((len(tile_sets), slot_total, tile_width, tile_width), jnp.bfloat16),
            pltpu.VMEM((source_total, tile_width, feat_width), jnp.bfloat16),
            *[pltpu.VMEM(out.shape, out.dtype) for out in out_shape],
            pltpu.VMEM((dest_blocks + 1, tile_width, feat_width), jnp.float32),
            pltpu.SemaphoreType.DMA((len(pieces) + len(tile_sets),)),
            pltpu.SemaphoreType.DMA((SIDE, SIDE + 1)),
        ],
        cost_estimate=pl.CostEstimate(
            flops=4 * slot_total * tile_width * tile_width * feat_width,
            bytes_accessed=source_total * tile_width * feat_width * 2 + tile_sets[0].size * 4 + dest_blocks * tile_width * feat_width * 2,
            transcendentals=0,
        ),
        compiler_params=pltpu.CompilerParams(vmem_limit_bytes=24 * 1024 * 1024),
    )(sources, targets, counts, place, degrees, *tile_sets, *pieces)
    return outs[:SIDE], outs[SIDE:]


def along_x(value, shift):
    pairs = [(i, i // SIDE * SIDE + (i % SIDE + shift) % SIDE) for i in range(SIDE * SIDE)]
    return lax.ppermute(value, "row", pairs)


def along_y_hi(value, shift):
    pairs = [(i, (i // SIDE + shift) % SIDE * SIDE + i % SIDE) for i in range(SIDE * SIDE)]
    return lax.ppermute(value, "row", pairs)


def along_blk(value, moved):
    def index(y_lo, z, core):
        return (y_lo * RING + z % RING) * PAIR + core

    pairs = [
        (index(y_lo, z, core), index(*moved(y_lo, z, core)))
        for y_lo in range(PAIR)
        for z in range(RING)
        for core in range(PAIR)
    ]
    return lax.ppermute(value, "blk", pairs)


def to_other_y_lo(value):
    return along_blk(value, lambda y_lo, z, core: (1 - y_lo, z, core))


def to_other_core(value):
    return along_blk(value, lambda y_lo, z, core: (y_lo, z, 1 - core))


def along_z(value, shift):
    return along_blk(value, lambda y_lo, z, core: (y_lo, z + shift, core))


def wide(value):
    return value.astype(jnp.float32)


ORDER = (2, 1, 3)


def shifted_sums(parts, move):
    total = wide(parts[0])
    for shift in ORDER:
        got = move(parts[shift], shift)
        total += wide(got)
    return total


def reduce_scatter(first_parts, second_parts):
    narrow = jnp.bfloat16
    first = shifted_sums(first_parts, along_x).astype(narrow)
    second = shifted_sums(second_parts, along_y_hi).astype(narrow)
    first = shifted_sums([first[shift] for shift in range(SIDE)], along_y_hi)
    second = shifted_sums([second[:, shift] for shift in range(SIDE)], along_x)
    return first, second


def gather(features, meta, tiles, y_lo):
    node_rows, feat_width = features.shape
    half = feat_width // PAIR
    mine = lax.dynamic_slice_in_dim(features, y_lo * half, half, 1)
    theirs = lax.dynamic_slice_in_dim(features, (1 - y_lo) * half, half, 1)
    got = to_other_y_lo(theirs)
    other_meta = to_other_y_lo(meta)
    other_tiles = to_other_y_lo(tiles)
    own = jnp.concatenate([mine, got], axis=0)

    def swapped(values):
        value = jnp.concatenate(values, axis=0)
        return value, to_other_core(value)

    m2, p2 = along_z(own, 2), along_z(own, -2)
    m1, p1 = along_z(own, 1), along_z(own, -1)
    m3, p3 = along_z(m2, 1), along_z(p2, -1)
    opposite = [along_z(m2[:node_rows], 2), along_z(p2[node_rows:], -2)]
    near = swapped([own, p1, m1])
    p2, m2 = swapped([p2]), swapped([m2])
    far = swapped([p3, m3] + opposite)
    pieces = [part[at] for at in range(PAIR) for part in (near, p2, m2, far)]
    return pieces, other_meta, other_tiles


Z_ORDER = (0, 1, RING - 1, 2, RING - 2, 3, RING - 3, RING // 2)


def table_block(sources, y_lo, z, core, inner_total):
    inner, position = sources % inner_total, sources // inner_total
    place = [Z_ORDER.index(distance) for distance in range(RING)]
    away = (position // PAIR - z) % RING
    along = sum(jnp.where(away == distance, place[distance], 0) for distance in range(RING))
    other_core = position % PAIR != core
    other_y_lo = position // (PAIR * RING) != y_lo
    return ((other_core * RING + along) * PAIR + other_y_lo) * inner_total + inner


def per_device(features, edge_tiles, tile_src, tile_dst, tile_count, weight, out_bias):
    tiles_here = edge_tiles[0, 0]
    source_ids = tile_src[0, 0]
    target_ids = tile_dst[0, 0]
    live_count = tile_count[0, 0]
    slot_total = tiles_here.shape[0]
    tile_width = tiles_here.shape[-1]
    node_rows, feat_width = features.shape
    group_count = lax.axis_size("row")
    dest_blocks = group_count * node_rows // tile_width
    slot_ids = jnp.arange(slot_total, dtype=jnp.int32)
    me = lax.axis_index("blk")
    y_lo, z, core = me // (RING * PAIR), me // PAIR % RING, me % PAIR
    row = lax.axis_index("row")
    place = jnp.stack([row % SIDE, row // SIDE]).astype(jnp.int32)

    meta = jnp.stack([source_ids, target_ids, jnp.full_like(source_ids, live_count)])
    meta = jnp.pad(meta, ((0, 5), (0, tile_width - slot_total)))
    pieces, other_meta, other_tiles = gather(features, meta, tiles_here, y_lo)
    other_meta = other_meta[:3, :slot_total]
    sources = jnp.stack([source_ids, other_meta[0]])
    counts = jnp.stack([live_count, other_meta[2, 0]])
    blocks_of = jnp.stack([y_lo, 1 - y_lo]) * dest_blocks
    live = slot_ids[None, :] < counts[:, None]
    targets = jnp.where(
        live, jnp.stack([target_ids, other_meta[1]]) + blocks_of[:, None], PAIR * dest_blocks
    )
    blocks = table_block(sources, y_lo, z, core, node_rows // tile_width)

    row_sums = jnp.sum(tiles_here, axis=2, dtype=jnp.float32)
    block_ids = jnp.arange(dest_blocks, dtype=jnp.int32)
    selector = (target_ids[None, :] == block_ids[:, None]) & (slot_ids < live_count)[None, :]
    degree_part = jnp.dot(selector.astype(jnp.float32), row_sums, precision=lax.Precision.HIGHEST)

    first_parts, second_parts = partial_sums(
        pieces,
        (tiles_here, other_tiles),
        blocks.astype(jnp.int32),
        targets.astype(jnp.int32),
        counts.astype(jnp.int32),
        place,
        degree_part.reshape(group_count, node_rows),
        node_rows,
    )
    first_parts, features_here = lax.optimization_barrier((first_parts, features))
    own_part = jnp.dot(features_here, weight[:feat_width], preferred_element_type=jnp.float32) + out_bias
    first, second = reduce_scatter(first_parts, second_parts)
    others = node_rows - FIRST
    totals = jnp.concatenate([first, second[:, :others]], axis=1)
    at_low = y_lo == 0
    degree = jnp.where(at_low, second[0, others], second[1, others])
    mine = jnp.where(at_low, totals[0], totals[1])
    theirs = to_other_y_lo(jnp.where(at_low, totals[1], totals[0]).astype(jnp.bfloat16))
    theirs = wide(theirs)
    aggregate = jnp.concatenate([jnp.where(at_low, mine, theirs), jnp.where(at_low, theirs, mine)], axis=1)
    neighbor_mean = (aggregate / jnp.maximum(degree, 1.0)[:, None]).astype(jnp.bfloat16)
    mixed = jnp.dot(neighbor_mean, weight[feat_width:], preferred_element_type=jnp.float32) + own_part
    return jax.nn.relu(mixed).astype(jnp.bfloat16)


def solution(mesh):
    in_specs = (
        P(("row", "blk"), None),
        P("row", "blk", None, None, None),
        P("row", "blk", None),
        P("row", "blk", None),
        P("row", "blk"),
        P(),
        P(),
    )

    return jax.shard_map(per_device, mesh=mesh, in_specs=in_specs, out_specs=P(("row", "blk"), None), check_vma=False)
```

```python
import jax
import jax.numpy as jnp
from jax import lax
from jax.experimental import pallas as pl
from jax.experimental.pallas import tpu as pltpu
from jax.sharding import PartitionSpec as P


UNROLL = 16
SIDE, PAIR, RING = 4, 2, 8
FIRST = 176
EXTRA = 8


def partial_sums(pieces, tile_sets, sources, targets, counts, place, degrees, owner_rows):
    slot_total, tile_width, _ = tile_sets[0].shape
    feat_width = pieces[0].shape[-1]
    owner_blocks = owner_rows // tile_width
    dest_blocks = SIDE * SIDE * PAIR * owner_blocks
    pieces = [piece.reshape(-1, tile_width, feat_width) for piece in pieces]
    source_total = sum(piece.shape[0] for piece in pieces)

    def kernel(src_ref, dst_ref, count_ref, place_ref, degree_ref, *refs):
        sets, refs = refs[: len(tile_sets)], refs[len(tile_sets) :]
        piece_refs, refs = refs[: len(pieces)], refs[len(pieces) :]
        outs, (tiles_ref, table_ref, total_ref, in_sems) = refs[: 2 * SIDE], refs[2 * SIDE :]
        loads, base = [], 0
        for piece_ref in piece_refs:
            loads.append((piece_ref, table_ref.at[pl.ds(base, piece_ref.shape[0])]))
            base += piece_ref.shape[0]
        loads += [(set_ref, tiles_ref.at[at]) for at, set_ref in enumerate(sets)]
        loads = [pltpu.make_async_copy(*pair, in_sems.at[at]) for at, pair in enumerate(loads)]
        for load in loads:
            load.start()

        def clear(block, carry):
            total_ref[block] = jnp.zeros((tile_width, feat_width), jnp.float32)
            return carry

        lax.fori_loop(0, dest_blocks, clear, 0)
        for load in loads:
            load.wait()

        for at in range(len(sets)):

            def some_slots(index, carry):
                slots = [index * UNROLL + step for step in range(UNROLL)]
                products = [
                    jnp.dot(tiles_ref[at, slot], table_ref[src_ref[at, slot]], preferred_element_type=jnp.float32)
                    for slot in slots
                ]
                for slot, product in zip(slots, products):
                    total_ref[dst_ref[at, slot]] += product
                return carry

            lax.fori_loop(0, pl.cdiv(count_ref[at], UNROLL), some_slots, 0)

        for y_shift in range(SIDE):
            owner_y = lax.rem(place_ref[1] + y_shift, SIDE)
            for x_shift in range(SIDE):
                owner = owner_y * SIDE + lax.rem(place_ref[0] + x_shift, SIDE)
                degree_row = jnp.broadcast_to(degree_ref[owner], (EXTRA, owner_rows)).astype(jnp.bfloat16)

                def round_once(y_lo, carry, x_shift=x_shift, y_shift=y_shift, owner_y=owner_y, owner=owner, degree_row=degree_row):
                    block = (y_lo * SIDE * SIDE + owner) * owner_blocks
                    rows = jnp.concatenate(
                        [total_ref[block + inner].astype(jnp.bfloat16) for inner in range(owner_blocks)], axis=0
                    )
                    outs[x_shift][y_shift, y_lo] = rows[:FIRST]
                    outs[SIDE + y_shift][y_lo, x_shift, : owner_rows - FIRST] = rows[FIRST:]
                    outs[SIDE + y_shift][y_lo, x_shift, owner_rows - FIRST :] = degree_row
                    return carry

                lax.fori_loop(0, PAIR, round_once, 0)

    smem = pl.BlockSpec(memory_space=pltpu.SMEM)
    anywhere = pl.BlockSpec(memory_space=pl.ANY)
    vmem = pl.BlockSpec(memory_space=pltpu.VMEM)
    out_shape = [jax.ShapeDtypeStruct((SIDE, PAIR, FIRST, feat_width), jnp.bfloat16)] * SIDE
    out_shape += [jax.ShapeDtypeStruct((PAIR, SIDE, owner_rows - FIRST + EXTRA, feat_width), jnp.bfloat16)] * SIDE
    outs = pl.pallas_call(
        kernel,
        name="partial_sums",
        out_shape=out_shape,
        in_specs=[smem] * 4 + [vmem] + [anywhere] * (len(tile_sets) + len(pieces)),
        out_specs=[vmem] * len(out_shape),
        scratch_shapes=[
            pltpu.VMEM((len(tile_sets), slot_total, tile_width, tile_width), jnp.bfloat16),
            pltpu.VMEM((source_total, tile_width, feat_width), jnp.bfloat16),
            pltpu.VMEM((dest_blocks + 1, tile_width, feat_width), jnp.float32),
            pltpu.SemaphoreType.DMA((len(pieces) + len(tile_sets),)),
        ],
        cost_estimate=pl.CostEstimate(
            flops=4 * slot_total * tile_width * tile_width * feat_width,
            bytes_accessed=source_total * tile_width * feat_width * 2 + tile_sets[0].size * 4 + dest_blocks * tile_width * feat_width * 2,
            transcendentals=0,
        ),
        compiler_params=pltpu.CompilerParams(vmem_limit_bytes=18 * 1024 * 1024),
    )(sources, targets, counts, place, degrees, *tile_sets, *pieces)
    return outs[:SIDE], outs[SIDE:]


def along_x(value, shift):
    pairs = [(i, i // SIDE * SIDE + (i % SIDE + shift) % SIDE) for i in range(SIDE * SIDE)]
    return lax.ppermute(value, "row", pairs)


def along_y_hi(value, shift):
    pairs = [(i, (i // SIDE + shift) % SIDE * SIDE + i % SIDE) for i in range(SIDE * SIDE)]
    return lax.ppermute(value, "row", pairs)


def along_blk(value, moved):
    def index(y_lo, z, core):
        return (y_lo * RING + z % RING) * PAIR + core

    pairs = [
        (index(y_lo, z, core), index(*moved(y_lo, z, core)))
        for y_lo in range(PAIR)
        for z in range(RING)
        for core in range(PAIR)
    ]
    return lax.ppermute(value, "blk", pairs)


def to_other_y_lo(value):
    return along_blk(value, lambda y_lo, z, core: (1 - y_lo, z, core))


def to_other_core(value):
    return along_blk(value, lambda y_lo, z, core: (y_lo, z, 1 - core))


def wide(value):
    return value.astype(jnp.float32)


ORDER = (2, 1, 3)


def shifted_sums(parts, move):
    total = wide(parts[0])
    for shift in ORDER:
        got = move(parts[shift], shift)
        total += wide(got)
    return total


def reduce_scatter(first_parts, second_parts):
    narrow = jnp.bfloat16
    first = shifted_sums(first_parts, along_x).astype(narrow)
    second = shifted_sums(second_parts, along_y_hi).astype(narrow)
    first = shifted_sums([first[shift] for shift in range(SIDE)], along_y_hi)
    second = shifted_sums([second[:, shift] for shift in range(SIDE)], along_x)
    return first, second


def gather(features, meta, tiles, y_lo):
    node_rows, feat_width = features.shape
    half = feat_width // PAIR
    mine = lax.dynamic_slice_in_dim(features, y_lo * half, half, 1)
    theirs = lax.dynamic_slice_in_dim(features, (1 - y_lo) * half, half, 1)
    got = to_other_y_lo(theirs)
    other_meta = to_other_y_lo(meta)
    other_tiles = to_other_y_lo(tiles)
    own = jnp.concatenate([mine, got], axis=0)

    def passed(value, steps):
        return along_blk(value, lambda y_lo, z, core: (y_lo, z + (steps if core == 0 else -steps), core))

    at_0 = jnp.concatenate([own, to_other_core(own)], axis=0)
    at_2, at_1 = passed(at_0, 2), passed(at_0, 1)
    at_4, at_3 = passed(at_2[: PAIR * node_rows], 2), passed(at_2, 1)
    others = [to_other_core(at) for at in (at_1, at_2, at_3, at_4)]
    return [at_0, at_1, at_2, at_3, at_4] + others, other_meta, other_tiles


def table_block(sources, y_lo, z, core, inner_total):
    inner, position = sources % inner_total, sources // inner_total
    other_core = (position % PAIR != core).astype(jnp.int32)
    other_y_lo = (position // (PAIR * RING) != y_lo).astype(jnp.int32)
    away = position // PAIR - z
    away = jnp.where(core == 0, -away, away) % RING
    middle = RING // 2
    slot = jnp.where(
        away < middle,
        PAIR * away + other_core,
        jnp.where(
            away == middle,
            jnp.where(other_core == 0, PAIR * middle, PAIR * RING - 1),
            PAIR * (RING - away) + middle * PAIR - 1 + (1 - other_core),
        ),
    )
    return (slot * PAIR + other_y_lo) * inner_total + inner


def per_device(features, edge_tiles, tile_src, tile_dst, tile_count, weight, out_bias):
    tiles_here = edge_tiles[0, 0]
    source_ids = tile_src[0, 0]
    target_ids = tile_dst[0, 0]
    live_count = tile_count[0, 0]
    slot_total = tiles_here.shape[0]
    tile_width = tiles_here.shape[-1]
    node_rows, feat_width = features.shape
    group_count = lax.axis_size("row")
    dest_blocks = group_count * node_rows // tile_width
    slot_ids = jnp.arange(slot_total, dtype=jnp.int32)
    me = lax.axis_index("blk")
    y_lo, z, core = me // (RING * PAIR), me // PAIR % RING, me % PAIR
    row = lax.axis_index("row")
    place = jnp.stack([row % SIDE, row // SIDE]).astype(jnp.int32)

    meta = jnp.stack([source_ids, target_ids, jnp.full_like(source_ids, live_count)])
    meta = jnp.pad(meta, ((0, 5), (0, tile_width - slot_total)))
    pieces, other_meta, other_tiles = gather(features, meta, tiles_here, y_lo)
    other_meta = other_meta[:3, :slot_total]
    sources = jnp.stack([source_ids, other_meta[0]])
    counts = jnp.stack([live_count, other_meta[2, 0]])
    blocks_of = jnp.stack([y_lo, 1 - y_lo]) * dest_blocks
    live = slot_ids[None, :] < counts[:, None]
    targets = jnp.where(
        live, jnp.stack([target_ids, other_meta[1]]) + blocks_of[:, None], PAIR * dest_blocks
    )
    blocks = table_block(sources, y_lo, z, core, node_rows // tile_width)

    row_sums = jnp.sum(tiles_here, axis=2, dtype=jnp.float32)
    block_ids = jnp.arange(dest_blocks, dtype=jnp.int32)
    selector = (target_ids[None, :] == block_ids[:, None]) & (slot_ids < live_count)[None, :]
    degree_part = jnp.dot(selector.astype(jnp.float32), row_sums, precision=lax.Precision.HIGHEST)

    first_parts, second_parts = partial_sums(
        pieces,
        (tiles_here, other_tiles),
        blocks.astype(jnp.int32),
        targets.astype(jnp.int32),
        counts.astype(jnp.int32),
        place,
        degree_part.reshape(group_count, node_rows),
        node_rows,
    )
    first_parts, features_here = lax.optimization_barrier((first_parts, features))
    own_part = jnp.dot(features_here, weight[:feat_width], preferred_element_type=jnp.float32) + out_bias
    first, second = reduce_scatter(first_parts, second_parts)
    others = node_rows - FIRST
    totals = jnp.concatenate([first, second[:, :others]], axis=1)
    at_low = y_lo == 0
    degree = jnp.where(at_low, second[0, others], second[1, others])
    mine = jnp.where(at_low, totals[0], totals[1])
    theirs = to_other_y_lo(jnp.where(at_low, totals[1], totals[0]).astype(jnp.bfloat16))
    theirs = wide(theirs)
    aggregate = jnp.concatenate([jnp.where(at_low, mine, theirs), jnp.where(at_low, theirs, mine)], axis=1)
    neighbor_mean = (aggregate / jnp.maximum(degree, 1.0)[:, None]).astype(jnp.bfloat16)
    mixed = jnp.dot(neighbor_mean, weight[feat_width:], preferred_element_type=jnp.float32) + own_part
    return jax.nn.relu(mixed).astype(jnp.bfloat16)


def solution(mesh):
    in_specs = (
        P(("row", "blk"), None),
        P("row", "blk", None, None, None),
        P("row", "blk", None),
        P("row", "blk", None),
        P("row", "blk"),
        P(),
        P(),
    )

    return jax.shard_map(per_device, mesh=mesh, in_specs=in_specs, out_specs=P(("row", "blk"), None), check_vma=False)
```
